128 devices in a mesh: row: 8 (over x, core), col: 16 (over z, y).
Axes of the slice: x: 4, y: 4, z: 4, core: 2. Of those that a mesh axis runs over, the one named last changes fastest.
Arguments:
- density_tiles: float32 [3, 4096, 4096], P(None, ('row', 'col')), may hold values from -0.012 to 0.012
- tile_ids: int32 [4096], P(('row', 'col')), may hold values from 0 to 16383, as said below
- batch_blocks: int32 [128, 8], replicated, may hold values from 0 to 127, as said below
- basis_values: float32 [128, 512, 1024], P(('row', 'col')), may hold values from -6 to 6
- grid_weight: float32 [128, 1024], P(('row', 'col')), may hold values from 0.0002 to 0.002
- xc_kernel: float32 [128, 1024], P(('row', 'col')), may hold values from -2 to -0.5
- grid_coord: float32 [3, 128, 1024], P(None, ('row', 'col')), may hold values from -1 to 1
- orbitals: float32 [8192, 512], P('row'), may hold values from -1.5 to 1.5
- precond_diag: float32 [8192], P('row'), may hold values from 1 to 4
- orbital_energy: float32 [512], replicated, may hold values from -3 to -0.5
Outputs:
- new_density: float32 [3, 4096, 4096], P(None, ('row', 'col'))
The draws below stay inside these ranges and needn't reach their ends.
Inputs may be any that keep to these rules, and one draw needn't show every extreme that they name: `tile_ids`: the 32 slots of device (r, c), counted in row+col order, list distinct tiles I * 128 + J with I in the r-th range of 16 blocks and J in the c-th range of 8 blocks. `batch_blocks`: each row holds 8 ascending blocks, no two in the same range of 8 blocks, and exactly 1 of them in each range of 16 blocks.
All inputs are finite; a program needn't handle non-finite values.
Results may differ from the reference program's by a relative error of at most 0.0003.
Values sent between devices are 32-bit elements; how exact they have to be, the bound alone decides.
A program may use at most 128 MiB of HBM per device.

```python
import math
import jax
import jax.numpy as jnp
from jax import lax

NB = 8192
TILE = 64
NOCC = 512
PTS = 1024
FB = 8
TPD = 32
NBLK = 128
ROWBLK = 16
COLBLK = 8
NBATCH = 128
TILES = 4096
N_ROW = 8
N_COL = 16


def draw_tile_ids(key, part):
    key_list = jax.random.split(jax.random.fold_in(key, 11), N_ROW * N_COL)

    def device_tiles(device_key, device):
        local_tiles = jax.random.permutation(device_key, ROWBLK * COLBLK)[:TPD]
        row_index = device // N_COL
        col_index = device % N_COL
        block_row = row_index * ROWBLK + local_tiles // COLBLK
        block_col = col_index * COLBLK + local_tiles % COLBLK
        return block_row * NBLK + block_col
    listed = jax.vmap(device_tiles)(key_list, jnp.arange(N_ROW * N_COL, dtype=jnp.int32))
    return listed.reshape(-1).astype(jnp.int32)


def draw_batch_blocks(key, part):
    per_range = FB // N_ROW
    range_count = N_COL // N_ROW
    key_list = jax.random.split(jax.random.fold_in(key, 23), NBATCH * N_ROW)

    def choose_blocks(range_key):
        first_key, second_key = jax.random.split(range_key)
        chosen = jnp.sort(jax.random.permutation(first_key, range_count)[:per_range])
        offsets = jax.random.randint(second_key, (per_range,), 0, COLBLK)
        return chosen * COLBLK + offsets
    local_blocks = jax.vmap(choose_blocks)(key_list).reshape(NBATCH, N_ROW, per_range)
    row_start = (jnp.arange(N_ROW, dtype=jnp.int32) * ROWBLK)[None, :, None]
    return (local_blocks + row_start).reshape(NBATCH, FB).astype(jnp.int32)


def levels(stream_key, shape, shards, smallest, largest):
    gain = 1.0
    for position, parts in shards:
        steps = jax.random.uniform(jax.random.fold_in(jax.random.fold_in(stream_key, 6), position), (parts,), jnp.float32, smallest / len(shards), largest / len(shards))
        gain = gain * jnp.repeat(jnp.exp(steps), shape[position] // parts).reshape((-1,) + (1,) * (len(shape) - 1 - position))
    return gain


def bell_draw(key, extent, spread, limit, pieces=(), kind=jnp.bfloat16):
    values = spread * jax.random.normal(key, extent, jnp.float32)
    if pieces:
        values = values * levels(key, extent, pieces, -0.22, 0.18)
    return jnp.clip(values, -limit, limit).astype(kind)


def setup_inputs(seed: int = 0) -> dict:
    splits = jax.random.split(jax.random.key(seed), 11)
    density_tiles = bell_draw(splits[0], (3, TILES, TILE * TILE), 0.002, 0.012, ((1, 128),), jnp.float32)
    tile_ids = draw_tile_ids(jax.random.fold_in(splits[10], 71), 0)
    batch_blocks = draw_batch_blocks(jax.random.fold_in(splits[10], 71), 0)
    basis_values = bell_draw(splits[3], (NBATCH, FB * TILE, PTS), 1.0, 6.0, ((0, 128),), jnp.float32)
    grid_weight = jnp.clip(jnp.exp(math.log(0.002) - 2.3025852 * jax.random.uniform(splits[4], (NBATCH, PTS), jnp.float32) ** levels(splits[4], (NBATCH, PTS), ((0, 128),), -0.2, 0.2)), 0.0002, 0.002)
    xc_kernel = jnp.clip(-2.0 + 1.5 * jax.random.uniform(splits[5], (NBATCH, PTS), jnp.float32) ** levels(splits[5], (NBATCH, PTS), ((0, 128),), -0.2, 0.2), -2.0, -0.5)
    grid_coord = jnp.clip(jax.random.uniform(splits[6], (3, NBATCH, PTS), jnp.float32, -1.0, 1.0) * levels(splits[6], (3, NBATCH, PTS), ((1, 128),), -0.4, 0.0), -1.0, 1.0)
    orbitals = bell_draw(splits[7], (NB, NOCC), 0.25, 1.5, ((0, 8),), jnp.float32)
    precond_diag = jnp.clip(1.0 + 3.0 * jax.random.uniform(splits[8], (NB,), jnp.float32) ** levels(splits[8], (NB,), ((0, 8),), -0.2, 0.2), 1.0, 4.0)
    orbital_energy = jnp.clip(jax.random.uniform(splits[9], (NOCC,), jnp.float32, -3.0, -0.5), -3.0, -0.5)
    return {"density_tiles": density_tiles, "tile_ids": tile_ids, "batch_blocks": batch_blocks, "basis_values": basis_values, "grid_weight": grid_weight, "xc_kernel": xc_kernel, "grid_coord": grid_coord, "orbitals": orbitals, "precond_diag": precond_diag, "orbital_energy": orbital_energy}


PRECISE = lax.Precision.HIGHEST


def reference(density_tiles, tile_ids, batch_blocks, basis_values, grid_weight, xc_kernel, grid_coord, orbitals, precond_diag, orbital_energy):
    block_count = NB // TILE
    tile_total = tile_ids.shape[0]
    tile_area = TILE * TILE
    batch_width = FB * TILE
    slot_table = jnp.full((block_count * block_count,), tile_total, dtype=jnp.int32)
    slot_table = slot_table.at[tile_ids].set(jnp.arange(tile_total, dtype=jnp.int32))
    padded = jnp.concatenate([density_tiles, jnp.zeros((3, 1, tile_area), dtype=jnp.float32)], axis=1)

    def one_batch(running, inputs):
        blocks, values, weight, kernel, coords = inputs
        wanted = (blocks[:, None] * block_count + blocks[None, :]).reshape(-1).astype(jnp.int32)
        slot_ids = jnp.take(slot_table, wanted, axis=0).astype(jnp.int32)
        tile_data = jnp.take(padded, slot_ids, axis=1).reshape(3, FB, FB, TILE, TILE)
        density = tile_data.transpose(0, 1, 3, 2, 4).reshape(3, batch_width, batch_width)
        projected = jnp.einsum("dmn,np->dmp", density, values, precision=PRECISE)
        response = jnp.sum(values[None] * projected, axis=1)
        potential = kernel[None] * response + coords
        weighted = values[None] * (weight[None] * potential)[:, None, :]
        hamiltonian = jnp.einsum("dmp,np->dmn", weighted, values, precision=PRECISE)
        ham_tiles = hamiltonian.reshape(3, FB, TILE, FB, TILE).transpose(0, 1, 3, 2, 4).reshape(3, FB * FB, tile_area)
        return running.at[:, slot_ids].add(ham_tiles), None

    inputs = (batch_blocks, basis_values, grid_weight, xc_kernel, jnp.moveaxis(grid_coord, 1, 0))
    accumulated, _ = lax.scan(one_batch, jnp.zeros((3, tile_total + 1, tile_area), dtype=jnp.float32), inputs)
    group_size = TPD
    group_count = tile_total // group_size
    ham_groups = accumulated[:, :tile_total].reshape(3, group_count, group_size, TILE, TILE).transpose(1, 0, 2, 3, 4)
    row_ids = (tile_ids // block_count).astype(jnp.int32).reshape(group_count, group_size)
    col_ids = (tile_ids % block_count).astype(jnp.int32).reshape(group_count, group_size)
    orbital_blocks = orbitals.reshape(block_count, TILE, NOCC)

    def add_group(running, inputs):
        ham_group, group_rows, group_cols = inputs
        picked = jnp.take(orbital_blocks, group_cols, axis=0)
        products = jnp.einsum("dsab,sbo->dsao", ham_group, picked, precision=PRECISE)
        return running.at[:, group_rows].add(products), None

    projected_orbitals, _ = lax.scan(add_group, jnp.zeros((3, block_count, TILE, NOCC), dtype=jnp.float32), (ham_groups, row_ids, col_ids))
    denominator = precond_diag.reshape(block_count, TILE)[None, :, :, None] - orbital_energy[None, None, None, :]
    response_orbs = -projected_orbitals / denominator

    def new_group(inputs):
        group_rows, group_cols = inputs
        x_rows = jnp.take(response_orbs, group_rows, axis=1)
        x_cols = jnp.take(response_orbs, group_cols, axis=1)
        c_rows = jnp.take(orbital_blocks, group_rows, axis=0)
        c_cols = jnp.take(orbital_blocks, group_cols, axis=0)
        renewed = jnp.einsum("dsao,sbo->dsab", x_rows, c_cols, precision=PRECISE)
        renewed = renewed + jnp.einsum("sao,dsbo->dsab", c_rows, x_cols, precision=PRECISE)
        return renewed.reshape(3, group_size, tile_area)

    renewed_all = lax.map(new_group, (row_ids, col_ids))
    return renewed_all.transpose(1, 0, 2, 3).reshape(3, tile_total, tile_area)
```

```python
import jax
import jax.numpy as jnp
from jax import lax
from jax.experimental import pallas as pl
from jax.experimental.pallas import tpu as pltpu
from jax.sharding import PartitionSpec as P

TILE = 64
NBLK = 128
F32 = jnp.float32
BF16 = jnp.bfloat16
NT = (((1,), (1,)), ((), ()))


def split(x):
    hi = x.astype(BF16)
    lo = (x - hi.astype(F32)).astype(BF16)
    return hi, lo


def dot(a, b):
    return jnp.dot(a, b, preferred_element_type=F32)


def dot_nt(a, b):
    return lax.dot_general(a, b, NT, preferred_element_type=F32)


def vmem():
    return pl.BlockSpec(memory_space=pltpu.VMEM)


def smem():
    return pl.BlockSpec(memory_space=pltpu.SMEM)


def select_kernel(slot_ref, tiles_ref, out_ref):
    count = out_ref.shape[0]

    def body(n, carry):
        slot = slot_ref[n]
        found = jnp.where(slot >= 0, 1.0, 0.0).astype(F32)
        picked = tiles_ref[:, jnp.maximum(slot, 0)]
        out_ref[n] = picked * found
        return carry

    lax.fori_loop(0, count, body, 0)


def select_tiles(slots, tiles):
    return pl.pallas_call(
        select_kernel,
        out_shape=jax.ShapeDtypeStruct((slots.shape[0], 3, 32, 128), F32),
        in_specs=[smem(), vmem()],
        out_specs=vmem(),
        name="select_tiles",
    )(slots, tiles)


def batch_kernel(
    col_ref, mask_ref, t_ref, b_ref, gw_ref, xc_ref, gc_ref, c_ref, out_ref,
    bperm, plane, bstack, bside, dcat, acat, hcat, ccat, pot,
):
    for i in range(8):
        rows = pl.ds(i * 64, 64)
        hi, lo = split(b_ref[0, rows, :])
        bstack[pl.ds(i * 64, 64), :] = hi
        bstack[pl.ds(512 + i * 64, 64), :] = hi
        bstack[pl.ds(1024 + i * 64, 64), :] = lo
        bside[rows, 0:1024] = hi
        bside[rows, 1024:2048] = hi
        bside[rows, 2048:3072] = lo
        for k in range(8):
            plane[k, rows, :] = b_ref[0, rows, k * 128 : k * 128 + 128]
        chi, clo = split(c_ref[i])
        ccat[pl.ds(i * 64, 64), :] = chi
        ccat[pl.ds(512 + i * 64, 64), :] = chi
        ccat[pl.ds(1024 + i * 64, 64), :] = clo

    for i in range(8):
        for p in range(2):
            for k in range(8):
                bperm[pl.ds(i * 64 + p * 32, 32), k * 128 : k * 128 + 128] = plane[
                    k, pl.ds(i * 64 + p, 32, stride=2), :
                ]

    lane = lax.broadcasted_iota(jnp.int32, (32, 128), 1)
    left = lane < 64

    def per_direction(d, carry):
        for i in range(8):
            for q in range(4):
                t0 = t_ref[i * 16 + col_ref[2 * q], d]
                t1 = t_ref[i * 16 + col_ref[2 * q + 1], d]
                even = jnp.where(left, t0, pltpu.roll(t1, 64, 1))
                odd = jnp.where(left, pltpu.roll(t0, 64, 1), t1)
                for p, part in ((0, even), (1, odd)):
                    hi, lo = split(part)
                    rows = pl.ds(i * 64 + p * 32, 32)
                    dcat[rows, q * 128 : q * 128 + 128] = hi
                    dcat[rows, 512 + q * 128 : 640 + q * 128] = lo
                    dcat[rows, 1024 + q * 128 : 1152 + q * 128] = hi
        for n in range(4):
            cols = slice(n * 256, n * 256 + 256)
            projected = dot(dcat[...], bstack[:, cols])
            response = jnp.sum(bperm[:, cols] * projected, axis=0, keepdims=True)
            potential = xc_ref[:, cols] * response + gc_ref[d, :, cols]
            pot[:, cols] = gw_ref[:, cols] * potential
        for i in range(8):
            rows = pl.ds(i * 64, 64)
            hi, lo = split(b_ref[0, rows, :] * pot[...])
            acat[rows, 0:1024] = hi
            acat[rows, 1024:2048] = lo
            acat[rows, 2048:3072] = hi
        for n in range(2):
            ham = dot_nt(acat[...], bside[n * 256 : n * 256 + 256, :])
            for i in range(8):
                part = ham[i * 64 : i * 64 + 64] * mask_ref[i : i + 1, n * 256 : n * 256 + 256]
                hi, lo = split(part)
                rows = pl.ds(i * 64, 64)
                hcat[rows, n * 256 : n * 256 + 256] = hi
                hcat[rows, 512 + n * 256 : 768 + n * 256] = lo
                hcat[rows, 1024 + n * 256 : 1280 + n * 256] = hi
        for n in range(2):
            product = dot(hcat[...], ccat[:, n * 256 : n * 256 + 256])
            for i in range(8):
                for g in range(4):
                    for q in range(2):
                        row = i * 64 + g * 16
                        out_ref[i * 16 + g * 4 + n * 2 + q, d] = product[
                            row : row + 16, q * 128 : q * 128 + 128
                        ]
        return carry

    lax.fori_loop(0, 3, per_direction, 0)


def batch_product(col, mask, tiles, basis, weight, kernel, coord, c_batch):
    return pl.pallas_call(
        batch_kernel,
        out_shape=jax.ShapeDtypeStruct((128, 3, 16, 128), F32),
        in_specs=[smem()] + [vmem()] * 7,
        out_specs=vmem(),
        scratch_shapes=[
            pltpu.VMEM((512, 1024), F32),
            pltpu.VMEM((8, 512, 128), F32),
            pltpu.VMEM((1536, 1024), BF16),
            pltpu.VMEM((512, 3072), BF16),
            pltpu.VMEM((512, 1536), BF16),
            pltpu.VMEM((512, 3072), BF16),
            pltpu.VMEM((512, 1536), BF16),
            pltpu.VMEM((1536, 512), BF16),
            pltpu.VMEM((1, 1024), F32),
        ],
        name="batch_product",
    )(col, mask, tiles, basis, weight, kernel, coord, c_batch)


def solve_kernel(place_ref, arrived_ref, diag_ref, energy_ref, out_ref):
    out_ref[...] = jnp.zeros_like(out_ref)

    def body(b, carry):
        place = place_ref[b]
        out_ref[place] = out_ref[place] + arrived_ref[b]
        return carry

    lax.fori_loop(0, arrived_ref.shape[0], body, 0)
    for k in range(out_ref.shape[0]):
        denominator = diag_ref[k] - energy_ref[...]
        out_ref[k] = -out_ref[k] / denominator[None]


def solve(place, arrived, diag, energy):
    return pl.pallas_call(
        solve_kernel,
        out_shape=jax.ShapeDtypeStruct((16, 3, 16, 128), F32),
        in_specs=[smem()] + [vmem()] * 3,
        out_specs=vmem(),
        name="solve",
    )(place, arrived, diag, energy)


def renew_kernel(
    row_ref, col_ref, xr_ref, xc_ref, cr_ref, cc_ref, out_ref,
    ccat, xccat, xrcat, crcat, dense,
):
    for k in range(8):
        rows = pl.ds(k * 64, 64)
        hi, lo = split(cc_ref[k])
        ccat[rows, 0:512] = hi
        ccat[rows, 512:1024] = hi
        ccat[rows, 1024:1536] = lo
    for k in range(16):
        rows = pl.ds(k * 64, 64)
        hi, lo = split(cr_ref[k])
        crcat[rows, 0:512] = hi
        crcat[rows, 512:1024] = lo
        crcat[rows, 1024:1536] = hi
    lane = lax.broadcasted_iota(jnp.int32, (32, 128), 1)
    left = lane < 64

    def per_direction(d, carry):
        for k in range(8):
            rows = pl.ds(k * 64, 64)
            hi, lo = split(xc_ref[k, d])
            xccat[rows, 0:512] = hi
            xccat[rows, 512:1024] = hi
            xccat[rows, 1024:1536] = lo
        for k in range(16):
            rows = pl.ds(k * 64, 64)
            hi, lo = split(xr_ref[k, d])
            xrcat[rows, 0:512] = hi
            xrcat[rows, 512:1024] = lo
            xrcat[rows, 1024:1536] = hi
        for m in range(4):
            rows = slice(m * 256, m * 256 + 256)
            for n in range(2):
                cols = slice(n * 256, n * 256 + 256)
                value = dot_nt(xrcat[rows, :], ccat[cols, :]) + dot_nt(
                    crcat[rows, :], xccat[cols, :]
                )
                dense[2 * n, rows, :] = value[:, 0:128]
                dense[2 * n + 1, rows, :] = value[:, 128:256]

        def per_slot(s, inner):
            col = col_ref[s]
            start = pl.multiple_of(row_ref[s] * 64, 64)
            half = col % 2
            even = dense[col // 2, pl.ds(start, 32, stride=2), :]
            odd = dense[col // 2, pl.ds(start + 1, 32, stride=2), :]
            even = jnp.where(half == 0, even, pltpu.roll(even, 64, 1))
            odd = jnp.where(half == 1, odd, pltpu.roll(odd, 64, 1))
            out_ref[d, s] = jnp.where(left, even, odd)
            return inner

        lax.fori_loop(0, 32, per_slot, 0)
        return carry

    lax.fori_loop(0, 3, per_direction, 0)


def renew(rows, cols, x_rows, x_cols, c_rows, c_cols):
    return pl.pallas_call(
        renew_kernel,
        out_shape=jax.ShapeDtypeStruct((3, 32, 32, 128), F32),
        in_specs=[smem()] * 2 + [vmem()] * 4,
        out_specs=vmem(),
        scratch_shapes=[
            pltpu.VMEM((512, 1536), BF16),
            pltpu.VMEM((512, 1536), BF16),
            pltpu.VMEM((1024, 1536), BF16),
            pltpu.VMEM((1024, 1536), BF16),
            pltpu.VMEM((4, 1024, 128), F32),
        ],
        name="renew",
    )(rows, cols, x_rows, x_cols, c_rows, c_cols)


def local(
    density_tiles,
    tile_ids,
    batch_blocks,
    basis_values,
    grid_weight,
    xc_kernel,
    grid_coord,
    orbitals,
    precond_diag,
    orbital_energy,
):
    row = lax.axis_index("row")
    col = lax.axis_index("col")
    me = row * 16 + col
    blocks = lax.dynamic_slice_in_dim(batch_blocks, me, 1, 0)[0]

    c_rows = orbitals.reshape(16, TILE, 512)
    asked = lax.dynamic_index_in_dim(batch_blocks.reshape(8, 16, 8), col, 1, keepdims=False)
    asked = lax.dynamic_index_in_dim(asked, row, 1, keepdims=False) - row * 16
    c_batch = lax.all_to_all(
        jnp.take(c_rows, asked, axis=0), "row", split_axis=0, concat_axis=0, tiled=True
    )
    piece = lax.dynamic_slice_in_dim(c_rows, (col % 2) * 8, 8, 0)
    c_cols = lax.psum(jnp.where(row == col // 2, piece, 0.0), "row")

    all_ids = lax.all_gather(tile_ids, ("row", "col"), tiled=True)
    wanted = (blocks[:, None] * NBLK + blocks[None, :]).reshape(-1)
    listed = jnp.any(wanted[:, None] == all_ids[None, :], axis=1).astype(F32).reshape(8, 8)
    mask = jnp.repeat(listed, TILE, axis=1)

    ask_row = lax.dynamic_index_in_dim(batch_blocks, row, 1, keepdims=False)
    ask_col = lax.dynamic_index_in_dim(batch_blocks, col // 2, 1, keepdims=False)
    match = (ask_row * NBLK + ask_col)[:, None] == tile_ids[None, :]
    slots = jnp.max(jnp.where(match, jnp.arange(32, dtype=jnp.int32)[None, :], -1), axis=1)
    outgoing = select_tiles(slots, density_tiles.reshape(3, 32, 32, 128))
    arrived = lax.all_to_all(outgoing, ("row", "col"), split_axis=0, concat_axis=0, tiled=True)

    product = batch_product(
        blocks // 8, mask, arrived, basis_values, grid_weight, xc_kernel, grid_coord, c_batch
    )
    spread = lax.all_to_all(product, ("row", "col"), split_axis=0, concat_axis=0, tiled=True)
    diag = lax.dynamic_index_in_dim(precond_diag.reshape(16, 4, 16), col // 4, 1, keepdims=False)
    energy = lax.dynamic_index_in_dim(orbital_energy.reshape(4, 128), col % 4, 0, keepdims=True)
    x_part = solve(
        ask_row - row * 16, spread, jnp.broadcast_to(diag[:, :, None], (16, 16, 128)), energy
    )
    x_all = lax.all_gather(x_part, "col").reshape(4, 4, 16, 3, 16, 128)
    x_rows = x_all.transpose(2, 3, 0, 4, 1, 5).reshape(16, 3, TILE, 512)
    x_piece = lax.dynamic_slice_in_dim(x_rows, (col % 2) * 8, 8, 0)
    x_cols = lax.psum(jnp.where(row == col // 2, x_piece, 0.0), "row")

    renewed = renew(
        tile_ids // NBLK - row * 16, tile_ids % NBLK - col * 8, x_rows, x_cols, c_rows, c_cols
    )
    return renewed.reshape(3, 32, TILE * TILE)


def solution(mesh):
    placed = (
        P(None, ("row", "col"), None),
        P(("row", "col")),
        P(),
        P(("row", "col"), None, None),
        P(("row", "col"), None),
        P(("row", "col"), None),
        P(None, ("row", "col"), None),
        P("row", None),
        P("row"),
        P(),
    )
    return jax.shard_map(
        local, mesh=mesh, in_specs=placed, out_specs=P(None, ("row", "col"), None), check_vma=False
    )
```

```python
import jax
import jax.numpy as jnp
from jax import lax
from jax.experimental import pallas as pl
from jax.experimental.pallas import tpu as pltpu
from jax.sharding import PartitionSpec as P

TILE = 64
NBLK = 128
F32 = jnp.float32
BF16 = jnp.bfloat16
NT = (((1,), (1,)), ((), ()))


def split(x):
    hi = x.astype(BF16)
    lo = (x - hi.astype(F32)).astype(BF16)
    return hi, lo


def dot(a, b):
    return jnp.dot(a, b, preferred_element_type=F32)


def dot_nt(a, b):
    return lax.dot_general(a, b, NT, preferred_element_type=F32)


def vmem():
    return pl.BlockSpec(memory_space=pltpu.VMEM)


def smem():
    return pl.BlockSpec(memory_space=pltpu.SMEM)


def select_kernel(slot_ref, tiles_ref, out_ref):
    count = out_ref.shape[0]

    def body(n, carry):
        slot = slot_ref[n]
        picked = tiles_ref[:, jnp.maximum(slot, 0)]
        out_ref[n] = jnp.where(slot >= 0, picked, jnp.inf)
        return carry

    lax.fori_loop(0, count, body, 0)


def select_tiles(slots, tiles):
    return pl.pallas_call(
        select_kernel,
        out_shape=jax.ShapeDtypeStruct((slots.shape[0], 3, 32, 128), F32),
        in_specs=[smem(), vmem()],
        out_specs=vmem(),
        name="select_tiles",
    )(slots, tiles)


def batch_kernel(
    col_ref, t_ref, b_ref, gw_ref, xc_ref, gc_ref, c_ref, out_ref,
    bperm, plane, bstack, bside, dcat, acat, hcat, ccat, pot, mask,
):
    for i in range(8):
        rows = pl.ds(i * 64, 64)
        hi, lo = split(b_ref[0, rows, :])
        bstack[pl.ds(i * 64, 64), :] = hi
        bstack[pl.ds(512 + i * 64, 64), :] = hi
        bstack[pl.ds(1024 + i * 64, 64), :] = lo
        bside[rows, 0:1024] = hi
        bside[rows, 1024:2048] = hi
        bside[rows, 2048:3072] = lo
        for k in range(8):
            plane[k, rows, :] = b_ref[0, rows, k * 128 : k * 128 + 128]
        chi, clo = split(c_ref[i])
        ccat[pl.ds(i * 64, 64), :] = chi
        ccat[pl.ds(512 + i * 64, 64), :] = chi
        ccat[pl.ds(1024 + i * 64, 64), :] = clo

    for i in range(8):
        for p in range(2):
            for k in range(8):
                bperm[pl.ds(i * 64 + p * 32, 32), k * 128 : k * 128 + 128] = plane[
                    k, pl.ds(i * 64 + p, 32, stride=2), :
                ]

    lane = lax.broadcasted_iota(jnp.int32, (32, 128), 1)
    left = lane < 64

    def per_direction(d, carry):
        for i in range(8):
            for q in range(4):
                t0 = t_ref[i * 16 + col_ref[2 * q], d]
                t1 = t_ref[i * 16 + col_ref[2 * q + 1], d]
                listed0 = t0 < jnp.inf
                listed1 = t1 < jnp.inf
                t0 = jnp.where(listed0, t0, 0.0)
                t1 = jnp.where(listed1, t1, 0.0)
                mask[i : i + 1, q * 128 : q * 128 + 128] = jnp.where(
                    left[0:1],
                    jnp.where(listed0[0:1], 1.0, 0.0),
                    jnp.where(listed1[0:1], 1.0, 0.0),
                )
                even = jnp.where(left, t0, pltpu.roll(t1, 64, 1))
                odd = jnp.where(left, pltpu.roll(t0, 64, 1), t1)
                for p, part in ((0, even), (1, odd)):
                    hi, lo = split(part)
                    rows = pl.ds(i * 64 + p * 32, 32)
                    dcat[rows, q * 128 : q * 128 + 128] = hi
                    dcat[rows, 512 + q * 128 : 640 + q * 128] = lo
                    dcat[rows, 1024 + q * 128 : 1152 + q * 128] = hi
        for n in range(4):
            cols = slice(n * 256, n * 256 + 256)
            projected = dot(dcat[...], bstack[:, cols])
            response = jnp.sum(bperm[:, cols] * projected, axis=0, keepdims=True)
            potential = xc_ref[:, cols] * response + gc_ref[d, :, cols]
            pot[:, cols] = gw_ref[:, cols] * potential
        for i in range(8):
            rows = pl.ds(i * 64, 64)
            hi, lo = split(b_ref[0, rows, :] * pot[...])
            acat[rows, 0:1024] = hi
            acat[rows, 1024:2048] = lo
            acat[rows, 2048:3072] = hi
        for n in range(2):
            ham = dot_nt(acat[...], bside[n * 256 : n * 256 + 256, :])
            for i in range(8):
                part = ham[i * 64 : i * 64 + 64] * mask[i : i + 1, n * 256 : n * 256 + 256]
                hi, lo = split(part)
                rows = pl.ds(i * 64, 64)
                hcat[rows, n * 256 : n * 256 + 256] = hi
                hcat[rows, 512 + n * 256 : 768 + n * 256] = lo
                hcat[rows, 1024 + n * 256 : 1280 + n * 256] = hi
        for n in range(2):
            product = dot(hcat[...], ccat[:, n * 256 : n * 256 + 256])
            for i in range(8):
                for g in range(4):
                    for q in range(2):
                        row = i * 64 + g * 16
                        out_ref[i * 16 + g * 4 + n * 2 + q, d] = product[
                            row : row + 16, q * 128 : q * 128 + 128
                        ]
        return carry

    lax.fori_loop(0, 3, per_direction, 0)


def batch_product(col, tiles, basis, weight, kernel, coord, c_batch):
    return pl.pallas_call(
        batch_kernel,
        out_shape=jax.ShapeDtypeStruct((128, 3, 16, 128), F32),
        in_specs=[smem()] + [vmem()] * 6,
        out_specs=vmem(),
        scratch_shapes=[
            pltpu.VMEM((512, 1024), F32),
            pltpu.VMEM((8, 512, 128), F32),
            pltpu.VMEM((1536, 1024), BF16),
            pltpu.VMEM((512, 3072), BF16),
            pltpu.VMEM((512, 1536), BF16),
            pltpu.VMEM((512, 3072), BF16),
            pltpu.VMEM((512, 1536), BF16),
            pltpu.VMEM((1536, 512), BF16),
            pltpu.VMEM((1, 1024), F32),
            pltpu.VMEM((8, 512), F32),
        ],
        name="batch_product",
    )(col, tiles, basis, weight, kernel, coord, c_batch)


def solve_kernel(place_ref, arrived_ref, diag_ref, energy_ref, out_ref):
    out_ref[...] = jnp.zeros_like(out_ref)

    def body(b, carry):
        place = place_ref[b]
        out_ref[place] = out_ref[place] + arrived_ref[b]
        return carry

    lax.fori_loop(0, arrived_ref.shape[0], body, 0)
    for k in range(out_ref.shape[0]):
        denominator = diag_ref[k] - energy_ref[...]
        out_ref[k] = -out_ref[k] / denominator[None]


def solve(place, arrived, diag, energy):
    return pl.pallas_call(
        solve_kernel,
        out_shape=jax.ShapeDtypeStruct((16, 3, 16, 128), F32),
        in_specs=[smem()] + [vmem()] * 3,
        out_specs=vmem(),
        name="solve",
    )(place, arrived, diag, energy)


MESH = pl.DeviceIdType.MESH


def spread_kernel(
    x_ref, c_ref, rows_ref, cols_ref,
    own_sem, ring_send, ring_recv, scatter_send, scatter_recv, line_send, line_recv,
):
    row = lax.axis_index("row")
    col = lax.axis_index("col")
    z, y = col // 4, col % 4
    x, core = row // 2, row % 2
    home = col // 2 == row

    def across(axis, step):
        if axis == 0:
            return (row, lax.rem(z + step + 4, 4) * 4 + y)
        return (row, z * 4 + lax.rem(y + step + 4, 4))

    def along(step):
        return (lax.rem(x + step + 4, 4) * 2 + core, col)

    partner = (x * 2 + 1 - core, col)

    barrier = pltpu.get_barrier_semaphore()
    for device in (
        across(0, 1), across(0, -1), across(1, 1), across(1, -1), along(1), along(-1), partner
    ):
        pl.semaphore_signal(barrier, inc=1, device_id=device, device_id_type=MESH)

    def greet(k, carry):
        @pl.when(jnp.logical_or(col // 2 != row, k != col))
        def _():
            pl.semaphore_signal(barrier, inc=1, device_id=(col // 2, k), device_id_type=MESH)

        return carry

    lax.fori_loop(0, 16, greet, 0)
    pl.semaphore_wait(barrier, 23 - home.astype(jnp.int32))

    def remote(src, dst, send, recv, device):
        return pltpu.make_async_remote_copy(
            src_ref=src, dst_ref=dst, send_sem=send, recv_sem=recv,
            device_id=device, device_id_type=MESH,
        )

    def window(ref, block, planes, oz, oy):
        return ref.at[
            block, planes,
            pl.ds(pl.multiple_of(oz * 16, 16), 16), pl.ds(pl.multiple_of(oy * 128, 128), 128),
        ]

    def scatter(k, h):
        return remote(
            x_ref.at[h * 8 + k], window(cols_ref, k, pl.ds(0, 3), z, y),
            scatter_send.at[h * 8 + k], scatter_recv, (k, row * 2 + h),
        )

    def scatter_orbitals(k):
        return remote(
            c_ref.at[(col % 2) * 8 + k], cols_ref.at[k, 3],
            scatter_send.at[16 + k], scatter_recv, (k, col),
        )

    def start_scatter(k, carry):
        for h in range(2):
            here = jnp.logical_and(k == row, row * 2 + h == col)

            @pl.when(here)
            def _():
                pltpu.make_async_copy(
                    x_ref.at[h * 8 + k], window(cols_ref, k, pl.ds(0, 3), z, y), scatter_recv
                ).start()

            @pl.when(jnp.logical_not(here))
            def _():
                scatter(k, h).start()

        @pl.when(jnp.logical_and(home, k == row))
        def _():
            pltpu.make_async_copy(
                c_ref.at[(col % 2) * 8 + k], cols_ref.at[k, 3], scatter_recv
            ).start()

        @pl.when(jnp.logical_and(home, k != row))
        def _():
            scatter_orbitals(k).start()

        return carry

    lax.fori_loop(0, 8, start_scatter, 0)

    def spot(half, first, second, blocks):
        oz, oy = (z + second, y + first) if half == 0 else (z + first, y + second)
        lo, count = blocks
        return window(
            rows_ref, pl.ds(half * 8 + lo, count), pl.ds(0, 3),
            lax.rem(oz + 8, 4), lax.rem(oy + 8, 4),
        )

    ALL, LOW, HIGH = (0, 8), (0, 4), (4, 4)

    def hop(half, phase, index, first, second, blocks, step):
        axis = (1, 0)[half] if phase == 0 else (0, 1)[half]
        if first == 0 and second == 0:
            src = x_ref.at[pl.ds(half * 8, 8)]
        else:
            src = spot(half, first, second, blocks)
        return remote(
            src, spot(half, first, second, blocks),
            ring_send.at[half, index], ring_recv.at[half, index], across(axis, step),
        )

    ORIGINS = (0, -1, 1, 2)
    sent = []

    def go(*args):
        copy = hop(*args)
        copy.start()
        sent.append(copy)

    def arrive(half, phase, index, first, second, blocks):
        hop(half, phase, index, first, second, blocks, 1).wait_recv()

    own = [
        pltpu.make_async_copy(
            x_ref.at[pl.ds(half * 8, 8)], spot(half, 0, 0, ALL), own_sem.at[half]
        )
        for half in range(2)
    ]
    for half in range(2):
        go(half, 0, 0, 0, 0, ALL, 1)
        go(half, 0, 1, 0, 0, ALL, -1)
    for half in range(2):
        go(half, 1, 4, 0, 0, ALL, 1)
        go(half, 1, 5, 0, 0, ALL, -1)
        own[half].start()

    pltpu.make_async_copy(cols_ref.at[row], cols_ref.at[row], scatter_recv).wait()

    def line(index, distance, planes, device):
        block = lax.rem(x + distance + 4, 4) * 2 + core
        ref = cols_ref.at[block, planes]
        return remote(ref, ref, line_send.at[index], line_recv.at[index], device)

    def landed(index, distance, planes, other):
        owner = core if other == 0 else 1 - core
        ref = cols_ref.at[lax.rem(x + distance + 4, 4) * 2 + owner, planes]
        remote(ref, ref, line_send.at[index], line_recv.at[index], partner).wait_recv()

    FULL, FRONT, BACK = pl.ds(0, 4), pl.ds(0, 2), pl.ds(2, 2)
    lines = []

    def pass_on(index, distance, planes, device):
        copy = line(index, distance, planes, device)
        copy.start()
        lines.append(copy)

    pass_on(0, 0, FULL, along(1))
    pass_on(1, 0, FULL, along(-1))
    pass_on(4, 0, FULL, partner)

    for half in range(2):
        arrive(half, 0, 0, -1, 0, ALL)
        go(half, 0, 2, -1, 0, LOW, 1)
        go(half, 1, 6, -1, 0, ALL, 1)
        go(half, 1, 7, -1, 0, ALL, -1)
        arrive(half, 0, 1, 1, 0, ALL)
        go(half, 0, 3, 1, 0, HIGH, -1)
        go(half, 1, 8, 1, 0, ALL, 1)
        go(half, 1, 9, 1, 0, ALL, -1)
    landed(0, -1, FULL, 0)
    pass_on(2, -1, FRONT, along(1))
    pass_on(5, -1, FULL, partner)
    landed(1, 1, FULL, 0)
    pass_on(3, 1, BACK, along(-1))
    pass_on(6, 1, FULL, partner)
    for half in range(2):
        arrive(half, 0, 2, 2, 0, LOW)
        arrive(half, 0, 3, 2, 0, HIGH)
        go(half, 1, 10, 2, 0, ALL, 1)
        go(half, 1, 11, 2, 0, ALL, -1)
    for k, first in enumerate(ORIGINS):
        for half in range(2):
            arrive(half, 1, 4 + 2 * k, first, -1, ALL)
            go(half, 1, 12 + 2 * k, first, -1, LOW, 1)
            arrive(half, 1, 5 + 2 * k, first, 1, ALL)
            go(half, 1, 13 + 2 * k, first, 1, HIGH, -1)
        if k == 1:
            landed(2, 2, FRONT, 0)
            landed(3, 2, BACK, 0)
            pass_on(7, 2, FULL, partner)
    for k, first in enumerate(ORIGINS):
        for half in range(2):
            arrive(half, 1, 12 + 2 * k, first, 2, LOW)
            arrive(half, 1, 13 + 2 * k, first, 2, HIGH)
    landed(4, 0, FULL, 1)
    landed(5, -1, FULL, 1)
    landed(6, 1, FULL, 1)
    landed(7, 2, FULL, 1)
    for copy in own:
        copy.wait()
    for copy in sent + lines:
        copy.wait_send()

    def finish_scatter(k, carry):
        for h in range(2):
            @pl.when(jnp.logical_not(jnp.logical_and(k == row, row * 2 + h == col)))
            def _():
                scatter(k, h).wait_send()

        @pl.when(jnp.logical_and(home, k != row))
        def _():
            scatter_orbitals(k).wait_send()

        return carry

    lax.fori_loop(0, 8, finish_scatter, 0)


def spread_orbitals(x_part, c_rows):
    any_space = pl.BlockSpec(memory_space=pl.ANY)
    return pl.pallas_call(
        spread_kernel,
        out_shape=(
            jax.ShapeDtypeStruct((16, 3, TILE, 512), F32),
            jax.ShapeDtypeStruct((8, 4, TILE, 512), F32),
        ),
        in_specs=[any_space, any_space],
        out_specs=(any_space, any_space),
        scratch_shapes=[
            pltpu.SemaphoreType.DMA((2,)),
            pltpu.SemaphoreType.DMA((2, 20)),
            pltpu.SemaphoreType.DMA((2, 20)),
            pltpu.SemaphoreType.DMA((24,)),
            pltpu.SemaphoreType.DMA,
            pltpu.SemaphoreType.DMA((8,)),
            pltpu.SemaphoreType.DMA((8,)),
        ],
        compiler_params=pltpu.CompilerParams(collective_id=1, has_side_effects=True),
        name="spread_orbitals",
    )(x_part, c_rows)


def renew_kernel(
    row_ref, col_ref, xr_ref, xc_ref, cr_ref, out_ref,
    ccat, xccat, xrcat, crcat, dense,
):
    for k in range(8):
        rows = pl.ds(k * 64, 64)
        hi, lo = split(xc_ref[k, 3])
        ccat[rows, 0:512] = hi
        ccat[rows, 512:1024] = hi
        ccat[rows, 1024:1536] = lo
    for k in range(16):
        rows = pl.ds(k * 64, 64)
        hi, lo = split(cr_ref[k])
        crcat[rows, 0:512] = hi
        crcat[rows, 512:1024] = lo
        crcat[rows, 1024:1536] = hi
    lane = lax.broadcasted_iota(jnp.int32, (32, 128), 1)
    left = lane < 64

    def per_direction(d, carry):
        for k in range(8):
            rows = pl.ds(k * 64, 64)
            hi, lo = split(xc_ref[k, d])
            xccat[rows, 0:512] = hi
            xccat[rows, 512:1024] = hi
            xccat[rows, 1024:1536] = lo
        for k in range(16):
            rows = pl.ds(k * 64, 64)
            hi, lo = split(xr_ref[k, d])
            xrcat[rows, 0:512] = hi
            xrcat[rows, 512:1024] = lo
            xrcat[rows, 1024:1536] = hi
        for m in range(4):
            rows = slice(m * 256, m * 256 + 256)
            for n in range(2):
                cols = slice(n * 256, n * 256 + 256)
                value = dot_nt(xrcat[rows, :], ccat[cols, :]) + dot_nt(
                    crcat[rows, :], xccat[cols, :]
                )
                dense[2 * n, rows, :] = value[:, 0:128]
                dense[2 * n + 1, rows, :] = value[:, 128:256]

        def per_slot(s, inner):
            col = col_ref[s]
            start = pl.multiple_of(row_ref[s] * 64, 64)
            half = col % 2
            even = dense[col // 2, pl.ds(start, 32, stride=2), :]
            odd = dense[col // 2, pl.ds(start + 1, 32, stride=2), :]
            even = jnp.where(half == 0, even, pltpu.roll(even, 64, 1))
            odd = jnp.where(half == 1, odd, pltpu.roll(odd, 64, 1))
            out_ref[d, s] = jnp.where(left, even, odd)
            return inner

        lax.fori_loop(0, 32, per_slot, 0)
        return carry

    lax.fori_loop(0, 3, per_direction, 0)


def renew(rows, cols, x_rows, x_cols, c_rows):
    return pl.pallas_call(
        renew_kernel,
        out_shape=jax.ShapeDtypeStruct((3, 32, 32, 128), F32),
        in_specs=[smem()] * 2 + [vmem()] * 3,
        out_specs=vmem(),
        scratch_shapes=[
            pltpu.VMEM((512, 1536), BF16),
            pltpu.VMEM((512, 1536), BF16),
            pltpu.VMEM((1024, 1536), BF16),
            pltpu.VMEM((1024, 1536), BF16),
            pltpu.VMEM((4, 1024, 128), F32),
        ],
        name="renew",
    )(rows, cols, x_rows, x_cols, c_rows)


def local(
    density_tiles,
    tile_ids,
    batch_blocks,
    basis_values,
    grid_weight,
    xc_kernel,
    grid_coord,
    orbitals,
    precond_diag,
    orbital_energy,
):
    row = lax.axis_index("row")
    col = lax.axis_index("col")
    me = row * 16 + col
    blocks = lax.dynamic_slice_in_dim(batch_blocks, me, 1, 0)[0]

    c_rows = orbitals.reshape(16, TILE, 512)
    asked = lax.dynamic_index_in_dim(batch_blocks.reshape(8, 16, 8), col, 1, keepdims=False)
    asked = lax.dynamic_index_in_dim(asked, row, 1, keepdims=False) - row * 16
    c_batch = lax.all_to_all(
        jnp.take(c_rows, asked, axis=0), "row", split_axis=0, concat_axis=0, tiled=True
    )
    ask_row = lax.dynamic_index_in_dim(batch_blocks, row, 1, keepdims=False)
    ask_col = lax.dynamic_index_in_dim(batch_blocks, col // 2, 1, keepdims=False)
    match = (ask_row * NBLK + ask_col)[:, None] == tile_ids[None, :]
    slots = jnp.max(jnp.where(match, jnp.arange(32, dtype=jnp.int32)[None, :], -1), axis=1)
    outgoing = select_tiles(slots, density_tiles.reshape(3, 32, 32, 128))
    arrived = lax.all_to_all(outgoing, ("row", "col"), split_axis=0, concat_axis=0, tiled=True)

    product = batch_product(
        blocks // 8, arrived, basis_values, grid_weight, xc_kernel, grid_coord, c_batch
    )
    spread = lax.all_to_all(product, ("row", "col"), split_axis=0, concat_axis=0, tiled=True)
    diag = lax.dynamic_index_in_dim(precond_diag.reshape(16, 4, 16), col // 4, 1, keepdims=False)
    energy = lax.dynamic_index_in_dim(orbital_energy.reshape(4, 128), col % 4, 0, keepdims=True)
    x_part = solve(
        ask_row - row * 16, spread, jnp.broadcast_to(diag[:, :, None], (16, 16, 128)), energy
    )
    x_rows, cols = spread_orbitals(x_part, c_rows)
    renewed = renew(tile_ids // NBLK - row * 16, tile_ids % NBLK - col * 8, x_rows, cols, c_rows)
    return renewed.reshape(3, 32, TILE * TILE)


def solution(mesh):
    placed = (
        P(None, ("row", "col"), None),
        P(("row", "col")),
        P(),
        P(("row", "col"), None, None),
        P(("row", "col"), None),
        P(("row", "col"), None),
        P(None, ("row", "col"), None),
        P("row", None),
        P("row"),
        P(),
    )
    return jax.shard_map(
        local, mesh=mesh, in_specs=placed, out_specs=P(None, ("row", "col"), None), check_vma=False
    )
```

```python
import jax
import jax.numpy as jnp
from jax import lax
from jax.experimental import pallas as pl
from jax.experimental.pallas import tpu as pltpu
from jax.sharding import PartitionSpec as P

TILE = 64
NBLK = 128
F32 = jnp.float32
BF16 = jnp.bfloat16
NT = (((1,), (1,)), ((), ()))


def split(x):
    hi = x.astype(BF16)
    lo = (x - hi.astype(F32)).astype(BF16)
    return hi, lo


def dot(a, b):
    return jnp.dot(a, b, preferred_element_type=F32)


def dot_nt(a, b):
    return lax.dot_general(a, b, NT, preferred_element_type=F32)


def vmem():
    return pl.BlockSpec(memory_space=pltpu.VMEM)


def smem():
    return pl.BlockSpec(memory_space=pltpu.SMEM)


MESH = pl.DeviceIdType.MESH


def gather_kernel(
    slot_ref, asked_ref, tiles_ref, c_ref, out_ref, cout_ref,
    mate0, mate1, mate2, picked, chosen,
    mate_send, mate_recv, tile_send, tile_recv, c_send, c_recv,
):
    row = lax.axis_index("row")
    col = lax.axis_index("col")
    z, y = col // 4, col % 4
    mates = (mate0, mate1, mate2)
    mate = (row, z * 4 + (y // 2) * 2 + 1 - y % 2)
    place = row * 8 + col // 2

    def target(n):
        t, rest = n % 2, n // 2
        tz, tr = lax.rem(z + rest % 4, 4), lax.rem(row + rest // 4, 8)
        return tr, tz * 4 + (1 - t) * y + t * (3 - y)

    barrier = pltpu.get_barrier_semaphore()
    pl.semaphore_signal(barrier, inc=1, device_id=mate, device_id_type=MESH)

    def greet(n, carry):
        pl.semaphore_signal(barrier, inc=1, device_id=target(n), device_id_type=MESH)
        return carry

    lax.fori_loop(1, 64, greet, 0)
    for k in range(8):
        chosen[k] = c_ref[asked_ref[k]]
    pl.semaphore_wait(barrier, 64)

    exchange = [
        pltpu.make_async_remote_copy(
            src_ref=tiles_ref.at[d], dst_ref=mates[d], send_sem=mate_send.at[d],
            recv_sem=mate_recv.at[d], device_id=mate, device_id_type=MESH,
        )
        for d in range(3)
    ]
    for copy in exchange:
        copy.start()

    def orbital_copy(k):
        to = lax.rem(row + k, 8)
        return pltpu.make_async_remote_copy(
            src_ref=chosen.at[to], dst_ref=cout_ref.at[row], send_sem=c_send.at[k],
            recv_sem=c_recv, device_id=(to, col), device_id_type=MESH,
        )

    own_orbitals = pltpu.make_async_copy(chosen.at[row], cout_ref.at[row], c_recv)
    own_orbitals.start()
    for k in range(1, 8):
        orbital_copy(k).start()

    def tile_copy(n, d):
        return pltpu.make_async_remote_copy(
            src_ref=picked.at[d, n], dst_ref=out_ref.at[place, d], send_sem=tile_send.at[d],
            recv_sem=tile_recv, device_id=target(n), device_id_type=MESH,
        )

    for d in range(3):
        exchange[d].wait_recv()

        def pick(n, carry):
            slot = slot_ref[n]
            own = tiles_ref[d, jnp.clip(slot, 0, 31)]
            other = mates[d][jnp.clip(slot - 32, 0, 31)]
            value = jnp.where(slot < 32, own, other)
            picked[d, n] = jnp.where(slot >= 0, value, jnp.inf)
            return carry

        lax.fori_loop(0, 64, pick, 0)
        pltpu.make_async_copy(picked.at[d, 0], out_ref.at[place, d], tile_recv).start()

        def send(n, carry):
            tile_copy(n, d).start()
            return carry

        lax.fori_loop(1, 64, send, 0)

    pltpu.make_async_copy(out_ref, out_ref, tile_recv).wait()
    pltpu.make_async_copy(cout_ref, cout_ref, c_recv).wait()
    for d in range(3):
        exchange[d].wait_send()
        rest = picked.at[d, pl.ds(1, 63)]
        pltpu.make_async_copy(rest, rest, tile_send.at[d]).wait()
    for k in range(1, 8):
        orbital_copy(k).wait_send()


def gather_tiles(slots, asked, tiles, c_rows):
    return pl.pallas_call(
        gather_kernel,
        out_shape=(
            jax.ShapeDtypeStruct((64, 3, 32, 128), F32),
            jax.ShapeDtypeStruct((8, TILE, 512), F32),
        ),
        in_specs=[smem(), smem(), vmem(), vmem()],
        out_specs=(pl.BlockSpec(memory_space=pl.ANY), pl.BlockSpec(memory_space=pl.ANY)),
        scratch_shapes=[
            pltpu.VMEM((32, 32, 128), F32),
            pltpu.VMEM((32, 32, 128), F32),
            pltpu.VMEM((32, 32, 128), F32),
            pltpu.VMEM((3, 64, 32, 128), F32),
            pltpu.VMEM((8, TILE, 512), F32),
            pltpu.SemaphoreType.DMA((3,)),
            pltpu.SemaphoreType.DMA((3,)),
            pltpu.SemaphoreType.DMA((3,)),
            pltpu.SemaphoreType.DMA,
            pltpu.SemaphoreType.DMA((8,)),
            pltpu.SemaphoreType.DMA,
        ],
        compiler_params=pltpu.CompilerParams(collective_id=0, has_side_effects=True),
        name="gather_tiles",
    )(slots, asked, tiles, c_rows)


def batch_kernel(
    t_ref, b_ref, gw_ref, xc_ref, gc_ref, c_ref, out_ref,
    bperm, plane, bstack, bside, dcat, acat, hcat, ccat, pot, mask,
):
    for i in range(8):
        rows = pl.ds(i * 64, 64)
        hi, lo = split(b_ref[0, rows, :])
        bstack[pl.ds(i * 64, 64), :] = hi
        bstack[pl.ds(512 + i * 64, 64), :] = hi
        bstack[pl.ds(1024 + i * 64, 64), :] = lo
        bside[rows, 0:1024] = hi
        bside[rows, 1024:2048] = hi
        bside[rows, 2048:3072] = lo
        for k in range(8):
            plane[k, rows, :] = b_ref[0, rows, k * 128 : k * 128 + 128]
        chi, clo = split(c_ref[i])
        ccat[pl.ds(i * 64, 64), :] = chi
        ccat[pl.ds(512 + i * 64, 64), :] = chi
        ccat[pl.ds(1024 + i * 64, 64), :] = clo

    for i in range(8):
        for p in range(2):
            for k in range(8):
                bperm[pl.ds(i * 64 + p * 32, 32), k * 128 : k * 128 + 128] = plane[
                    k, pl.ds(i * 64 + p, 32, stride=2), :
                ]

    lane = lax.broadcasted_iota(jnp.int32, (32, 128), 1)
    left = lane < 64

    def per_direction(d, carry):
        for i in range(8):
            for q in range(4):
                t0 = t_ref[i * 8 + 2 * q, d]
                t1 = t_ref[i * 8 + 2 * q + 1, d]
                listed0 = t0 < jnp.inf
                listed1 = t1 < jnp.inf
                t0 = jnp.where(listed0, t0, 0.0)
                t1 = jnp.where(listed1, t1, 0.0)
                mask[i : i + 1, q * 128 : q * 128 + 128] = jnp.where(
                    left[0:1],
                    jnp.where(listed0[0:1], 1.0, 0.0),
                    jnp.where(listed1[0:1], 1.0, 0.0),
                )
                even = jnp.where(left, t0, pltpu.roll(t1, 64, 1))
                odd = jnp.where(left, pltpu.roll(t0, 64, 1), t1)
                for p, part in ((0, even), (1, odd)):
                    hi, lo = split(part)
                    rows = pl.ds(i * 64 + p * 32, 32)
                    dcat[rows, q * 128 : q * 128 + 128] = hi
                    dcat[rows, 512 + q * 128 : 640 + q * 128] = lo
                    dcat[rows, 1024 + q * 128 : 1152 + q * 128] = hi
        for n in range(4):
            cols = slice(n * 256, n * 256 + 256)
            projected = dot(dcat[...], bstack[:, cols])
            response = jnp.sum(bperm[:, cols] * projected, axis=0, keepdims=True)
            potential = xc_ref[:, cols] * response + gc_ref[d, :, cols]
            pot[:, cols] = gw_ref[:, cols] * potential
        for i in range(8):
            rows = pl.ds(i * 64, 64)
            hi, lo = split(b_ref[0, rows, :] * pot[...])
            acat[rows, 0:1024] = hi
            acat[rows, 1024:2048] = lo
            acat[rows, 2048:3072] = hi
        for n in range(2):
            ham = dot_nt(acat[...], bside[n * 256 : n * 256 + 256, :])
            for i in range(8):
                part = ham[i * 64 : i * 64 + 64] * mask[i : i + 1, n * 256 : n * 256 + 256]
                hi, lo = split(part)
                rows = pl.ds(i * 64, 64)
                hcat[rows, n * 256 : n * 256 + 256] = hi
                hcat[rows, 512 + n * 256 : 768 + n * 256] = lo
                hcat[rows, 1024 + n * 256 : 1280 + n * 256] = hi
        for n in range(2):
            product = dot(hcat[...], ccat[:, n * 256 : n * 256 + 256])
            for i in range(8):
                for g in range(4):
                    for q in range(2):
                        row = i * 64 + g * 16
                        out_ref[i * 16 + g * 4 + n * 2 + q, d] = product[
                            row : row + 16, q * 128 : q * 128 + 128
                        ]
        return carry

    lax.fori_loop(0, 3, per_direction, 0)


def batch_product(tiles, basis, weight, kernel, coord, c_batch):
    return pl.pallas_call(
        batch_kernel,
        out_shape=jax.ShapeDtypeStruct((128, 3, 16, 128), F32),
        in_specs=[vmem()] * 6,
        out_specs=vmem(),
        scratch_shapes=[
            pltpu.VMEM((512, 1024), F32),
            pltpu.VMEM((8, 512, 128), F32),
            pltpu.VMEM((1536, 1024), BF16),
            pltpu.VMEM((512, 3072), BF16),
            pltpu.VMEM((512, 1536), BF16),
            pltpu.VMEM((512, 3072), BF16),
            pltpu.VMEM((512, 1536), BF16),
            pltpu.VMEM((1536, 512), BF16),
            pltpu.VMEM((1, 1024), F32),
            pltpu.VMEM((8, 512), F32),
        ],
        name="batch_product",
    )(tiles, basis, weight, kernel, coord, c_batch)


def solve_kernel(place_ref, arrived_ref, diag_ref, energy_ref, out_ref):
    out_ref[...] = jnp.zeros_like(out_ref)

    def body(b, carry):
        place = place_ref[b]
        out_ref[place] = out_ref[place] + arrived_ref[b]
        return carry

    lax.fori_loop(0, arrived_ref.shape[0], body, 0)
    for k in range(out_ref.shape[0]):
        denominator = diag_ref[k] - energy_ref[...]
        out_ref[k] = -out_ref[k] / denominator[None]


def solve(place, arrived, diag, energy):
    return pl.pallas_call(
        solve_kernel,
        out_shape=jax.ShapeDtypeStruct((16, 3, 16, 128), F32),
        in_specs=[smem()] + [vmem()] * 3,
        out_specs=vmem(),
        name="solve",
    )(place, arrived, diag, energy)


def spread_kernel(
    x_ref, c_ref, rows_ref, cols_ref,
    own_sem, ring_send, ring_recv, scatter_send, scatter_recv, line_send, line_recv,
):
    row = lax.axis_index("row")
    col = lax.axis_index("col")
    z, y = col // 4, col % 4
    x, core = row // 2, row % 2
    home = col // 2 == row

    def across(axis, step):
        if axis == 0:
            return (row, lax.rem(z + step + 4, 4) * 4 + y)
        return (row, z * 4 + lax.rem(y + step + 4, 4))

    def along(step):
        return (lax.rem(x + step + 4, 4) * 2 + core, col)

    partner = (x * 2 + 1 - core, col)

    barrier = pltpu.get_barrier_semaphore()
    for device in (
        across(0, 1), across(0, -1), across(1, 1), across(1, -1), along(1), along(-1), partner
    ):
        pl.semaphore_signal(barrier, inc=1, device_id=device, device_id_type=MESH)

    def greet(k, carry):
        @pl.when(jnp.logical_or(col // 2 != row, k != col))
        def _():
            pl.semaphore_signal(barrier, inc=1, device_id=(col // 2, k), device_id_type=MESH)

        return carry

    lax.fori_loop(0, 16, greet, 0)
    pl.semaphore_wait(barrier, 23 - home.astype(jnp.int32))

    def remote(src, dst, send, recv, device):
        return pltpu.make_async_remote_copy(
            src_ref=src, dst_ref=dst, send_sem=send, recv_sem=recv,
            device_id=device, device_id_type=MESH,
        )

    def window(ref, block, planes, oz, oy):
        return ref.at[
            block, planes,
            pl.ds(pl.multiple_of(oz * 16, 16), 16), pl.ds(pl.multiple_of(oy * 128, 128), 128),
        ]

    def scatter(k, h):
        return remote(
            x_ref.at[h * 8 + k], window(cols_ref, k, pl.ds(0, 3), z, y),
            scatter_send.at[h * 8 + k], scatter_recv, (k, row * 2 + h),
        )

    def scatter_orbitals(k):
        return remote(
            c_ref.at[(col % 2) * 8 + k], cols_ref.at[k, 3],
            scatter_send.at[16 + k], scatter_recv, (k, col),
        )

    def start_scatter(k, carry):
        for h in range(2):
            here = jnp.logical_and(k == row, row * 2 + h == col)

            @pl.when(here)
            def _():
                pltpu.make_async_copy(
                    x_ref.at[h * 8 + k], window(cols_ref, k, pl.ds(0, 3), z, y), scatter_recv
                ).start()

            @pl.when(jnp.logical_not(here))
            def _():
                scatter(k, h).start()

        @pl.when(jnp.logical_and(home, k == row))
        def _():
            pltpu.make_async_copy(
                c_ref.at[(col % 2) * 8 + k], cols_ref.at[k, 3], scatter_recv
            ).start()

        @pl.when(jnp.logical_and(home, k != row))
        def _():
            scatter_orbitals(k).start()

        return carry

    lax.fori_loop(0, 8, start_scatter, 0)

    def spot(half, first, second, blocks):
        oz, oy = (z + second, y + first) if half == 0 else (z + first, y + second)
        lo, count = blocks
        return window(
            rows_ref, pl.ds(half * 8 + lo, count), pl.ds(0, 3),
            lax.rem(oz + 8, 4), lax.rem(oy + 8, 4),
        )

    ALL, LOW, HIGH = (0, 8), (0, 4), (4, 4)

    def hop(half, phase, index, first, second, blocks, step):
        axis = (1, 0)[half] if phase == 0 else (0, 1)[half]
        if first == 0 and second == 0:
            src = x_ref.at[pl.ds(half * 8, 8)]
        else:
            src = spot(half, first, second, blocks)
        return remote(
            src, spot(half, first, second, blocks),
            ring_send.at[half, index], ring_recv.at[half, index], across(axis, step),
        )

    ORIGINS = (0, -1, 1, 2)
    sent = []

    def go(*args):
        copy = hop(*args)
        copy.start()
        sent.append(copy)

    def arrive(half, phase, index, first, second, blocks):
        hop(half, phase, index, first, second, blocks, 1).wait_recv()

    own = [
        pltpu.make_async_copy(
            x_ref.at[pl.ds(half * 8, 8)], spot(half, 0, 0, ALL), own_sem.at[half]
        )
        for half in range(2)
    ]
    for half in range(2):
        go(half, 0, 0, 0, 0, ALL, 1)
        go(half, 0, 1, 0, 0, ALL, -1)
    for half in range(2):
        go(half, 1, 4, 0, 0, ALL, 1)
        go(half, 1, 5, 0, 0, ALL, -1)
        own[half].start()

    pltpu.make_async_copy(cols_ref.at[row], cols_ref.at[row], scatter_recv).wait()

    def line(index, distance, planes, device):
        block = lax.rem(x + distance + 4, 4) * 2 + core
        ref = cols_ref.at[block, planes]
        return remote(ref, ref, line_send.at[index], line_recv.at[index], device)

    def landed(index, distance, planes, other):
        owner = core if other == 0 else 1 - core
        ref = cols_ref.at[lax.rem(x + distance + 4, 4) * 2 + owner, planes]
        remote(ref, ref, line_send.at[index], line_recv.at[index], partner).wait_recv()

    FULL, FRONT, BACK = pl.ds(0, 4), pl.ds(0, 2), pl.ds(2, 2)
    lines = []

    def pass_on(index, distance, planes, device):
        copy = line(index, distance, planes, device)
        copy.start()
        lines.append(copy)

    pass_on(0, 0, FULL, along(1))
    pass_on(1, 0, FULL, along(-1))
    pass_on(4, 0, FULL, partner)

    for half in range(2):
        arrive(half, 0, 0, -1, 0, ALL)
        go(half, 0, 2, -1, 0, LOW, 1)
        go(half, 1, 6, -1, 0, ALL, 1)
        go(half, 1, 7, -1, 0, ALL, -1)
        arrive(half, 0, 1, 1, 0, ALL)
        go(half, 0, 3, 1, 0, HIGH, -1)
        go(half, 1, 8, 1, 0, ALL, 1)
        go(half, 1, 9, 1, 0, ALL, -1)
    landed(0, -1, FULL, 0)
    pass_on(2, -1, FRONT, along(1))
    pass_on(5, -1, FULL, partner)
    landed(1, 1, FULL, 0)
    pass_on(3, 1, BACK, along(-1))
    pass_on(6, 1, FULL, partner)
    for half in range(2):
        arrive(half, 0, 2, 2, 0, LOW)
        arrive(half, 0, 3, 2, 0, HIGH)
        go(half, 1, 10, 2, 0, ALL, 1)
        go(half, 1, 11, 2, 0, ALL, -1)
    for k, first in enumerate(ORIGINS):
        for half in range(2):
            arrive(half, 1, 4 + 2 * k, first, -1, ALL)
            go(half, 1, 12 + 2 * k, first, -1, LOW, 1)
            arrive(half, 1, 5 + 2 * k, first, 1, ALL)
            go(half, 1, 13 + 2 * k, first, 1, HIGH, -1)
        if k == 1:
            landed(2, 2, FRONT, 0)
            landed(3, 2, BACK, 0)
            pass_on(7, 2, FULL, partner)
    for k, first in enumerate(ORIGINS):
        for half in range(2):
            arrive(half, 1, 12 + 2 * k, first, 2, LOW)
            arrive(half, 1, 13 + 2 * k, first, 2, HIGH)
    landed(4, 0, FULL, 1)
    landed(5, -1, FULL, 1)
    landed(6, 1, FULL, 1)
    landed(7, 2, FULL, 1)
    for copy in own:
        copy.wait()
    for copy in sent + lines:
        copy.wait_send()

    def finish_scatter(k, carry):
        for h in range(2):
            @pl.when(jnp.logical_not(jnp.logical_and(k == row, row * 2 + h == col)))
            def _():
                scatter(k, h).wait_send()

        @pl.when(jnp.logical_and(home, k != row))
        def _():
            scatter_orbitals(k).wait_send()

        return carry

    lax.fori_loop(0, 8, finish_scatter, 0)


def spread_orbitals(x_part, c_rows):
    any_space = pl.BlockSpec(memory_space=pl.ANY)
    return pl.pallas_call(
        spread_kernel,
        out_shape=(
            jax.ShapeDtypeStruct((16, 3, TILE, 512), F32),
            jax.ShapeDtypeStruct((8, 4, TILE, 512), F32),
        ),
        in_specs=[any_space, any_space],
        out_specs=(any_space, any_space),
        scratch_shapes=[
            pltpu.SemaphoreType.DMA((2,)),
            pltpu.SemaphoreType.DMA((2, 20)),
            pltpu.SemaphoreType.DMA((2, 20)),
            pltpu.SemaphoreType.DMA((24,)),
            pltpu.SemaphoreType.DMA,
            pltpu.SemaphoreType.DMA((8,)),
            pltpu.SemaphoreType.DMA((8,)),
        ],
        compiler_params=pltpu.CompilerParams(collective_id=1, has_side_effects=True),
        name="spread_orbitals",
    )(x_part, c_rows)


def renew_kernel(
    row_ref, col_ref, xr_ref, xc_ref, cr_ref, out_ref,
    ccat, xccat, xrcat, crcat, dense,
):
    for k in range(8):
        rows = pl.ds(k * 64, 64)
        hi, lo = split(xc_ref[k, 3])
        ccat[rows, 0:512] = hi
        ccat[rows, 512:1024] = hi
        ccat[rows, 1024:1536] = lo
    for k in range(16):
        rows = pl.ds(k * 64, 64)
        hi, lo = split(cr_ref[k])
        crcat[rows, 0:512] = hi
        crcat[rows, 512:1024] = lo
        crcat[rows, 1024:1536] = hi
    lane = lax.broadcasted_iota(jnp.int32, (32, 128), 1)
    left = lane < 64

    def per_direction(d, carry):
        for k in range(8):
            rows = pl.ds(k * 64, 64)
            hi, lo = split(xc_ref[k, d])
            xccat[rows, 0:512] = hi
            xccat[rows, 512:1024] = hi
            xccat[rows, 1024:1536] = lo
        for k in range(16):
            rows = pl.ds(k * 64, 64)
            hi, lo = split(xr_ref[k, d])
            xrcat[rows, 0:512] = hi
            xrcat[rows, 512:1024] = lo
            xrcat[rows, 1024:1536] = hi
        for m in range(4):
            rows = slice(m * 256, m * 256 + 256)
            for n in range(2):
                cols = slice(n * 256, n * 256 + 256)
                value = dot_nt(xrcat[rows, :], ccat[cols, :]) + dot_nt(
                    crcat[rows, :], xccat[cols, :]
                )
                dense[2 * n, rows, :] = value[:, 0:128]
                dense[2 * n + 1, rows, :] = value[:, 128:256]

        def per_slot(s, inner):
            col = col_ref[s]
            start = pl.multiple_of(row_ref[s] * 64, 64)
            half = col % 2
            even = dense[col // 2, pl.ds(start, 32, stride=2), :]
            odd = dense[col // 2, pl.ds(start + 1, 32, stride=2), :]
            even = jnp.where(half == 0, even, pltpu.roll(even, 64, 1))
            odd = jnp.where(half == 1, odd, pltpu.roll(odd, 64, 1))
            out_ref[d, s] = jnp.where(left, even, odd)
            return inner

        lax.fori_loop(0, 32, per_slot, 0)
        return carry

    lax.fori_loop(0, 3, per_direction, 0)


def renew(rows, cols, x_rows, x_cols, c_rows):
    return pl.pallas_call(
        renew_kernel,
        out_shape=jax.ShapeDtypeStruct((3, 32, 32, 128), F32),
        in_specs=[smem()] * 2 + [vmem()] * 3,
        out_specs=vmem(),
        scratch_shapes=[
            pltpu.VMEM((512, 1536), BF16),
            pltpu.VMEM((512, 1536), BF16),
            pltpu.VMEM((1024, 1536), BF16),
            pltpu.VMEM((1024, 1536), BF16),
            pltpu.VMEM((4, 1024, 128), F32),
        ],
        name="renew",
    )(rows, cols, x_rows, x_cols, c_rows)


def local(
    density_tiles,
    tile_ids,
    batch_blocks,
    basis_values,
    grid_weight,
    xc_kernel,
    grid_coord,
    orbitals,
    precond_diag,
    orbital_energy,
):
    row = lax.axis_index("row")
    col = lax.axis_index("col")
    z, y = col // 4, col % 4
    c_rows = orbitals.reshape(16, TILE, 512)

    pairs = [(c, c // 2 * 2 + 1 - c % 2) for c in range(16)]
    union = jnp.concatenate([tile_ids, lax.ppermute(tile_ids, "col", pairs)])
    ask_row = lax.dynamic_index_in_dim(batch_blocks, row, 1, keepdims=False)
    ask_col = lax.dynamic_index_in_dim(batch_blocks, col // 2, 1, keepdims=False)
    match = (ask_row * NBLK + ask_col)[:, None] == union[None, :]
    slots = jnp.max(jnp.where(match, jnp.arange(64, dtype=jnp.int32)[None, :], -1), axis=1)
    n = jnp.arange(64, dtype=jnp.int32)
    served_row = (row + n // 8) % 8
    served_col = (z + n // 2 % 4) % 4 * 4 + jnp.where(n % 2 == 0, y, 3 - y)
    slots = jnp.take(slots, served_row * 16 + served_col)
    asked = lax.dynamic_index_in_dim(ask_row.reshape(8, 16), col, 1, keepdims=False) - row * 16

    arrived, c_batch = gather_tiles(slots, asked, density_tiles.reshape(3, 32, 32, 128), c_rows)
    product = batch_product(
        arrived, basis_values, grid_weight, xc_kernel, grid_coord, c_batch
    )
    spread = lax.all_to_all(product, ("row", "col"), split_axis=0, concat_axis=0, tiled=True)
    diag = lax.dynamic_index_in_dim(precond_diag.reshape(16, 4, 16), col // 4, 1, keepdims=False)
    energy = lax.dynamic_index_in_dim(orbital_energy.reshape(4, 128), col % 4, 0, keepdims=True)
    x_part = solve(
        ask_row - row * 16, spread, jnp.broadcast_to(diag[:, :, None], (16, 16, 128)), energy
    )
    x_rows, cols = spread_orbitals(x_part, c_rows)
    renewed = renew(tile_ids // NBLK - row * 16, tile_ids % NBLK - col * 8, x_rows, cols, c_rows)
    return renewed.reshape(3, 32, TILE * TILE)


def solution(mesh):
    placed = (
        P(None, ("row", "col"), None),
        P(("row", "col")),
        P(),
        P(("row", "col"), None, None),
        P(("row", "col"), None),
        P(("row", "col"), None),
        P(None, ("row", "col"), None),
        P("row", None),
        P("row"),
        P(),
    )
    return jax.shard_map(
        local, mesh=mesh, in_specs=placed, out_specs=P(None, ("row", "col"), None), check_vma=False
    )
```
